32 devices in a mesh: group: 2 (over x), seq: 16 (over z, y, core).
Axes of the slice: x: 2, y: 2, z: 4, core: 2. Of those that a mesh axis runs over, the one named last changes fastest.
Arguments:
- prefix_key: bfloat16 [4096, 2048], P(('group', 'seq')), parts along dimension 0, may hold values from -6 to 6
- prefix_value: bfloat16 [4096, 2048], P(('group', 'seq')), parts along dimension 0, may hold values from -6 to 6
- prefix_kappa: bfloat16 [4096, 2048], P(('group', 'seq')), parts along dimension 0, may hold values from -6 to 6
- prefix_decay: bfloat16 [4096, 2048], P(('group', 'seq')), parts along dimension 0, as said below
- prefix_learn: bfloat16 [4096, 2048], P(('group', 'seq')), parts along dimension 0, may hold values from 0.0049743652 to 0.049804688
- answer_query: bfloat16 [32, 4, 8, 2048], P(('group', 'seq')), parts along dimension 0, may hold values from -6 to 6
- answer_key: bfloat16 [32, 4, 8, 2048], P(('group', 'seq')), parts along dimension 0, may hold values from -6 to 6
- answer_value: bfloat16 [32, 4, 8, 2048], P(('group', 'seq')), parts along dimension 0, may hold values from -6 to 6
- answer_kappa: bfloat16 [32, 4, 8, 2048], P(('group', 'seq')), parts along dimension 0, may hold values from -6 to 6
- answer_decay: bfloat16 [32, 4, 8, 2048], P(('group', 'seq')), parts along dimension 0, as said below
- answer_learn: bfloat16 [32, 4, 8, 2048], P(('group', 'seq')), parts along dimension 0, may hold values from 0.0049743652 to 0.049804688
- doc_lengths: int32 [8], P('group'), parts along dimension 0, may hold values from 1 to 8, as said below
- question_doc: int32 [32], P(('group', 'seq')), parts along dimension 0, may hold values from 0 to 3
- choice_tokens: int32 [32, 4, 8], P(('group', 'seq')), parts along dimension 0, may hold values from 0 to 65535
- choice_lengths: int32 [32, 4], P(('group', 'seq')), parts along dimension 0, may hold values from 1 to 8, 20 in all within a row
- head_weight: bfloat16 [2048, 65536], P(None, 'seq')
Outputs:
- scores: float32 [32, 4], P(('group', 'seq')), parts along dimension 0
The draws below stay inside these ranges and needn't reach their ends.
There are 2 independent parts, one for each index of `group`. The reference program is written for one: setup_inputs(seed, part) draws one part's arguments, and reference() takes and returns one part's arrays. A program takes and returns all parts, laid end to end along the dimension named above; an argument that names none is the same for every part. Nothing has to cross between parts.
Inputs may be any that keep to these rules, and one draw needn't show every extreme that they name: `doc_lengths`: they sum to 16; the largest is exactly 8. `choice_lengths`: the lengths of one question's choices sum to 20, and the largest of them is exactly 8. `prefix_decay`: positive. `answer_decay`: positive.
All inputs are finite; a program needn't handle non-finite values.
Results may differ from the reference program's by a relative error of at most 0.0003.
The reference program's roundings to bfloat16 on the way (of `doc_state` and `hidden`) count: a program that leaves them out, or rounds other values in their place, can miss the bound.
Values may be sent and summed in bfloat16 or wider, within the bound.
A program may use at most 128 MiB of HBM per device.

```python
import math
import jax
import jax.numpy as jnp
import numpy as np
from jax import lax

HEADS = 32
HSIZE = 64
WIDTH = 2048
VOCAB = 65536
TOK_DEV = 128
QUEST_DEV = 1
CHOICES = 4
ANS_LEN = 8
QUESTIONS = 16
TOKENS = 2048
DOCS = 4
MOST_SPAN = 8
N_SEQ = 16


def rate_law(key, line_elements, block):
    attention_draw_seed, category_draw_seed, feature_draw_seed, segment_draw_seed, cluster_draw_seed = jax.random.split(key, 5)
    chain = float(MOST_SPAN * TOK_DEV)
    slow_low = math.log(0.1 / chain)
    slow_high = math.log(1.0 / chain)
    fast_share = 0.5
    head_pick = jax.random.uniform(attention_draw_seed, (HEADS,))
    slow_rate = jnp.exp(slow_low + (slow_high - slow_low) * head_pick)
    fast_rate = jnp.exp(math.log(1.0 / 50.0) + (math.log(1.0 / 30.0) - math.log(1.0 / 50.0)) * head_pick)
    fast_flag = jax.random.uniform(category_draw_seed, (HEADS,)) < fast_share
    head_rate = jnp.where(fast_flag, fast_rate, slow_rate)
    channel = jnp.exp(jax.random.uniform(feature_draw_seed, (line_elements, HEADS, HSIZE), minval=-0.7, maxval=0.7))
    blocks = line_elements // block
    shard_factor = jnp.exp(jax.random.uniform(segment_draw_seed, (blocks, 1, 1, 1), minval=-0.7, maxval=0.7))
    attribute_settings = head_rate[None, :, None] * channel
    attribute_settings = (attribute_settings.reshape(blocks, block, HEADS, HSIZE) * shard_factor).reshape(line_elements, HEADS, HSIZE)
    cluster_dispersion = jax.random.uniform(cluster_draw_seed, (line_elements, 1, 1)) < 4.0 / line_elements
    attribute_settings = attribute_settings + jnp.where(cluster_dispersion, 0.45, 0.0)
    return attribute_settings.reshape(line_elements, HEADS * HSIZE)


def draw_prefix_decay(key, part):
    line_elements = TOK_DEV * N_SEQ
    return rate_law(jax.random.fold_in(key, 11), line_elements, TOK_DEV).astype(jnp.bfloat16)


def draw_answer_decay(key, part):
    line_elements = QUEST_DEV * N_SEQ * CHOICES * ANS_LEN
    attribute_settings = rate_law(jax.random.fold_in(key, 23), line_elements, ANS_LEN)
    return attribute_settings.reshape(QUEST_DEV * N_SEQ, CHOICES, ANS_LEN, HEADS * HSIZE).astype(jnp.bfloat16)


def draw_doc_lengths(key, part):
    cut_seed, place_seed = jax.random.split(jax.random.fold_in(key, 53), 2)
    remainder = N_SEQ - MOST_SPAN
    candidates = jax.random.permutation(cut_seed, jnp.arange(1, remainder, dtype=jnp.int32))
    cuts = jnp.sort(candidates[:DOCS - 2])
    bounds = jnp.concatenate([jnp.zeros((1,), jnp.int32), cuts, jnp.full((1,), remainder, jnp.int32)])
    others = (bounds[1:] - bounds[:-1]).astype(jnp.int32)
    whole = jnp.concatenate([jnp.full((1,), MOST_SPAN, jnp.int32), others])
    offset = (jax.random.randint(place_seed, (), 0, DOCS) + part) % DOCS
    return jnp.roll(whole, offset).astype(jnp.int32)


def draw_head_weight(key, part):
    key_base = jax.random.fold_in(jax.random.fold_in(key, 37), 0)
    features = HEADS * HSIZE
    scale = 3.0 / math.sqrt(features)
    base = jax.random.normal(key_base, (features, VOCAB)) * scale
    return jnp.clip(base, -6.0 * scale, 6.0 * scale).astype(jnp.bfloat16)


def plant(entries, stream_key, least, largest):
    shape = entries.shape
    spot = [jax.random.randint(jax.random.fold_in(stream_key, axis), (), 0, shape[axis]) for axis in range(len(shape))]
    entries = entries.at[tuple(spot)].set(least)
    longest = shape.index(max(shape))
    spot[longest] = (spot[longest] + 1) % shape[longest]
    return entries.at[tuple(spot)].set(largest)


def block_scale(stream_key, dims, pieces, smallest, largest):
    gain, own = 1.0, jax.random.fold_in(stream_key, 6)
    for axis_at, shards_of in pieces:
        heights = jnp.exp(jax.random.uniform(jax.random.fold_in(own, axis_at), (shards_of,), jnp.float32, smallest / len(pieces), largest / len(pieces)))
        gain = gain * jnp.repeat(heights, dims[axis_at] // shards_of).reshape([-1 if axis == axis_at else 1 for axis in range(len(dims))])
    return gain


def cumulative_ranks(amount, slope):
    portions = [(1 << 20) // math.isqrt(rank ** slope) + 1 for rank in range(1, amount + 1)]
    deviation = 1 + sum(portions) // (1 << 30)
    return np.cumsum(np.array([max(1, weight // deviation) for weight in portions]))


def ranked(own_key, extent, number_of, skew):
    grid = cumulative_ranks(number_of, skew)
    lot = jax.random.randint(jax.random.fold_in(own_key, 1), extent, 0, int(grid[number_of - 1]))
    grade = jnp.searchsorted(jnp.asarray(grid, jnp.int32), lot, side="right")
    return jax.random.permutation(jax.random.fold_in(own_key, 2), number_of)[grade].astype(jnp.int32)


def profile(amount, total, bound, lean):
    loads = [(1 << 20) // math.isqrt(rank ** lean) + 1 for rank in range(2, amount + 1)]
    rest, counts = total - bound - (amount - 1), [1] * (amount - 1)
    while rest > 0:
        free = [i for i in range(amount - 1) if counts[i] < bound]
        mass, budget = sum([loads[i] for i in free]), rest
        for i in free:
            addition = min(bound - counts[i], max(1, budget * loads[i] // mass), rest)
            counts[i] = counts[i] + addition
            rest = rest - addition
    return np.array([bound] + counts)


def ragged_sizes(key, count, total, limit, skew):
    if count == 2:
        one = jax.random.randint(key, (), max(1, total - limit), min(limit, total - 1) + 1)
        return jnp.stack([one, total - one])
    tallies = jnp.asarray(profile(count, total, limit, skew), jnp.int32)
    pairs = (count - 1) // 2
    donor, sink = tallies[1:1 + 2 * pairs:2], tallies[2:2 + 2 * pairs:2]
    slack = jnp.minimum(donor - 1, limit - sink)
    passed = jax.random.randint(jax.random.fold_in(key, 1), (pairs,), 0, 1 << 20) % (slack + 1)
    tallies = tallies.at[1:1 + 2 * pairs:2].set(donor - passed).at[2:2 + 2 * pairs:2].set(sink + passed)
    return tallies[jax.random.permutation(jax.random.fold_in(key, 2), count)]


def bell_draw(own_key, extent, scale, most, shards=(), kind=jnp.bfloat16):
    factor_of = block_scale(own_key, extent, shards, -0.22, 0.18) if shards else 1.0
    values = jax.random.normal(own_key, extent, jnp.float32) * scale * factor_of
    return jnp.minimum(jnp.maximum(values, -most), most).astype(kind)


def setup_inputs(seed: int = 0, part: int = 0) -> dict:
    key_list = jax.random.split(jax.random.key(seed), 17)
    part_splits = jax.random.split(jax.random.fold_in(key_list[16], part), 17)
    prefix_key = bell_draw(part_splits[0], (TOKENS, WIDTH), 1.0, 6.0, ((0, 16),))
    prefix_value = bell_draw(part_splits[1], (TOKENS, WIDTH), 1.0, 6.0, ((0, 16),))
    prefix_kappa = bell_draw(part_splits[2], (TOKENS, WIDTH), 1.0, 6.0, ((0, 16),))
    prefix_decay = draw_prefix_decay(jax.random.fold_in(jax.random.fold_in(key_list[16], part), 71), part)
    prefix_learn = jnp.clip(jnp.exp(math.log(0.049804688) - 2.3038113 * jax.random.uniform(part_splits[4], (TOKENS, WIDTH), jnp.float32) ** block_scale(part_splits[4], (TOKENS, WIDTH), ((0, 16),), -0.2, 0.2)), 0.0049743652, 0.049804688).astype(jnp.bfloat16)
    answer_query = bell_draw(part_splits[5], (QUESTIONS, CHOICES, ANS_LEN, WIDTH), 1.0, 6.0, ((0, 16),))
    answer_key = bell_draw(part_splits[6], (QUESTIONS, CHOICES, ANS_LEN, WIDTH), 1.0, 6.0, ((0, 16),))
    answer_value = bell_draw(part_splits[7], (QUESTIONS, CHOICES, ANS_LEN, WIDTH), 1.0, 6.0, ((0, 16),))
    answer_kappa = bell_draw(part_splits[8], (QUESTIONS, CHOICES, ANS_LEN, WIDTH), 1.0, 6.0, ((0, 16),))
    answer_decay = draw_answer_decay(jax.random.fold_in(jax.random.fold_in(key_list[16], part), 71), part)
    answer_learn = jnp.clip(jnp.exp(math.log(0.049804688) - 2.3038113 * jax.random.uniform(part_splits[10], (QUESTIONS, CHOICES, ANS_LEN, WIDTH), jnp.float32) ** block_scale(part_splits[10], (QUESTIONS, CHOICES, ANS_LEN, WIDTH), ((0, 16),), -0.2, 0.2)), 0.0049743652, 0.049804688).astype(jnp.bfloat16)
    doc_lengths = draw_doc_lengths(jax.random.fold_in(jax.random.fold_in(key_list[16], part), 71), part)
    question_doc = plant(jax.random.randint(part_splits[12], (QUESTIONS,), 0, DOCS), jax.random.fold_in(part_splits[12], 1), 0, DOCS - 1).astype(jnp.int32)
    choice_tokens = plant(ranked(part_splits[13], (QUESTIONS, CHOICES, ANS_LEN), VOCAB, 2), jax.random.fold_in(part_splits[13], 3), 0, VOCAB - 1).astype(jnp.int32)
    choice_lengths = jax.vmap(lambda own: ragged_sizes(own, CHOICES, CHOICES * ANS_LEN * 5 // 8, ANS_LEN, 0))(jax.random.split(part_splits[14], QUESTIONS)).reshape((QUESTIONS, CHOICES)).astype(jnp.int32)
    head_weight = draw_head_weight(jax.random.fold_in(key_list[16], 71), part)
    return dict(prefix_key=prefix_key, prefix_value=prefix_value, prefix_kappa=prefix_kappa, prefix_decay=prefix_decay, prefix_learn=prefix_learn, answer_query=answer_query, answer_key=answer_key, answer_value=answer_value, answer_kappa=answer_kappa, answer_decay=answer_decay, answer_learn=answer_learn, doc_lengths=doc_lengths, question_doc=question_doc, choice_tokens=choice_tokens, choice_lengths=choice_lengths, head_weight=head_weight)


def split_heads(tensor):
    return tensor.astype(jnp.float32).reshape(tensor.shape[:-1] + (HEADS, HSIZE))

def transition(kappa, decay, learn):
    unit_kappa = kappa * lax.rsqrt(lax.optimization_barrier(jnp.sum(kappa * kappa, -1, keepdims=True)) + 1e-06)
    return (jnp.exp(-decay), unit_kappa, unit_kappa * learn)

def advance(memory, retain, unit_kappa, removal):
    projected = lax.optimization_barrier(jnp.sum(memory * unit_kappa[..., None, :], -1, keepdims=True))
    return memory * retain[..., None, :] - projected * removal[..., None, :]

def group_norm(values):
    centre = values - lax.optimization_barrier(jnp.mean(values, -1, keepdims=True))
    spread = lax.optimization_barrier(jnp.mean(centre * centre, -1, keepdims=True))
    return centre * lax.rsqrt(spread + 1e-05)

def reference(prefix_key, prefix_value, prefix_kappa, prefix_decay, prefix_learn, answer_query, answer_key, answer_value, answer_kappa, answer_decay, answer_learn, doc_lengths, question_doc, choice_tokens, choice_lengths, head_weight):
    doc_ends = jnp.cumsum(doc_lengths).astype(jnp.int32)
    doc_starts = (doc_ends - doc_lengths).astype(jnp.int32)
    shard_ids = jnp.arange(N_SEQ, dtype=jnp.int32)
    opened = jnp.any(doc_starts[None, :] == shard_ids[:, None], axis=1)

    def shaped(tensor):
        return tensor.reshape(N_SEQ, TOK_DEV, HEADS * HSIZE)

    def shard_step(memory, inputs):
        memory = jnp.where(inputs[0], jnp.float32(0.0), memory)

        def token_step(memory, token):
            key_now, value_now, kappa_now, decay_now, learn_now = [split_heads(tensor) for tensor in token]
            retain, unit_kappa, removal = transition(kappa_now, decay_now, learn_now)
            memory = advance(memory, retain, unit_kappa, removal) + value_now[:, :, None] * key_now[:, None, :]
            return (memory, None)
        memory, _ = lax.scan(token_step, memory, inputs[1:])
        return (memory, memory)
    start_memory = jnp.zeros((HEADS, HSIZE, HSIZE), jnp.float32)
    _, shard_end = lax.scan(shard_step, start_memory, (opened, shaped(prefix_key), shaped(prefix_value), shaped(prefix_kappa), shaped(prefix_decay), shaped(prefix_learn)))
    doc_state = shard_end[doc_ends - 1].astype(jnp.bfloat16)
    begin = doc_state[question_doc].astype(jnp.float32)
    memory = jnp.broadcast_to(begin[:, None], (QUESTIONS, CHOICES, HEADS, HSIZE, HSIZE))
    per_token = []
    for step in range(ANS_LEN):
        query_now = split_heads(answer_query[:, :, step])
        key_now = split_heads(answer_key[:, :, step])
        value_now = split_heads(answer_value[:, :, step])
        retain, unit_kappa, removal = transition(split_heads(answer_kappa[:, :, step]), split_heads(answer_decay[:, :, step]), split_heads(answer_learn[:, :, step]))
        memory = advance(memory, retain, unit_kappa, removal) + value_now[..., :, None] * key_now[..., None, :]
        per_token.append(lax.optimization_barrier(jnp.sum(memory * query_now[..., None, :], -1)))
    output = jnp.stack(per_token, 2)
    hidden = group_norm(output).reshape(QUESTIONS, CHOICES * ANS_LEN, HEADS * HSIZE).astype(jnp.bfloat16)

    def score_one(inputs):
        line_elements, targets = inputs
        logits = jnp.dot(line_elements, head_weight, preferred_element_type=jnp.float32)
        peak_logit = lax.optimization_barrier(jnp.max(logits, -1, keepdims=True))
        total = peak_logit[:, 0] + jnp.log(lax.optimization_barrier(jnp.sum(jnp.exp(logits - peak_logit), -1)))
        picked = jnp.take_along_axis(logits, targets[:, None], 1)[:, 0]
        return picked - total
    logprob = lax.map(score_one, (hidden, choice_tokens.reshape(QUESTIONS, CHOICES * ANS_LEN)))
    logprob = logprob.reshape(QUESTIONS, CHOICES, ANS_LEN)
    inside = jnp.arange(ANS_LEN, dtype=jnp.int32)[None, None, :] < choice_lengths[:, :, None]
    return lax.optimization_barrier(jnp.sum(jnp.where(inside, logprob, jnp.float32(0.0)), -1)) / choice_lengths.astype(jnp.float32)
```

```python
import functools

import jax
import jax.numpy as jnp
from jax import lax
from jax.experimental import pallas as pl
from jax.experimental.pallas import tpu as pltpu
from jax.sharding import PartitionSpec as P

HSIZE = 64
LANES = 128
WIDE = 256
F32 = jnp.float32
BF16 = jnp.bfloat16


def split(x):
    high = x.astype(BF16)
    return high, (x - high.astype(F32)).astype(BF16)


def mm(a, b, dims):
    return lax.dot_general(a, b, (dims, ((), ())), preferred_element_type=F32)


NN = ((1,), (0,))
TN = ((0,), (0,))
NT = ((1,), (1,))


def dot3(a, b, dims=NN):
    ah, al = split(a)
    bh, bl = split(b)
    rows = a.shape[0]
    if dims != TN and rows % 16 == 0:
        both = mm(jnp.concatenate([ah, al], 0), bh, dims)
        return both[:rows] + (both[rows:] + mm(ah, bl, dims))
    return mm(ah, bh, dims) + (mm(al, bh, dims) + mm(ah, bl, dims))


def block_mask(rows, cols):
    return (
        lax.broadcasted_iota(jnp.int32, (rows, cols), 0) // HSIZE
        == lax.broadcasted_iota(jnp.int32, (rows, cols), 1) // HSIZE
    )


def head_sum(x, ones):
    rows = x.shape[0]
    high, low = split(x)
    both = mm(jnp.concatenate([high, low], 0), ones, NN)
    return both[:rows] + both[rows:]


def stack_heads(x):
    heads = x.shape[1] // HSIZE
    lane = lax.broadcasted_iota(jnp.int32, x.shape, 1) // HSIZE
    return jnp.concatenate([jnp.where(lane == h, x, jnp.zeros_like(x)) for h in range(heads)], 0)


def fold_heads(x):
    heads = x.shape[1] // HSIZE
    out = x[:HSIZE]
    for h in range(1, heads):
        out = out + x[h * HSIZE : (h + 1) * HSIZE]
    return out


def factors(kappa, decay, learn, ones):
    kappa = kappa.astype(F32)
    unit = kappa * lax.rsqrt(head_sum(kappa * kappa, ones) + 1e-06)
    return jnp.exp(-decay.astype(F32)), unit, unit * learn.astype(F32)


def stack_split(x):
    heads = x.shape[1] // HSIZE
    lane = lax.broadcasted_iota(jnp.int32, (1, x.shape[1]), 1) // HSIZE
    keep = [jnp.where(lane == h, 1.0, 0.0).astype(BF16) for h in range(heads)]
    return [jnp.concatenate([part * k for k in keep], 0) for part in split(x)]


def dot_stacked(a, stacked, dims):
    rows = a.shape[0]
    both = mm(jnp.concatenate(split(a), 0), stacked[0], dims)
    return both[:rows] + (both[rows:] + mm(a.astype(BF16), stacked[1], dims))


def merge(gain, pulled, faded, keys, size):
    rows, wide = pulled.shape
    pairs = rows // (2 * size)
    half = rows // 2

    def parted(x):
        x = x.reshape(pairs, 2, size, wide)
        return x[:, 0].reshape(half, wide), x[:, 1].reshape(half, wide)

    def joined(x, y):
        shape = (pairs, 1, size, wide)
        return jnp.concatenate([x.reshape(shape), y.reshape(shape)], 1).reshape(rows, wide)

    def scaled(x, by):
        return (x.reshape(pairs, size, wide) * by).reshape(half, wide)

    gain = gain.reshape(pairs, 2, 1, wide)
    gain_a, gain_b = gain[:, 0], gain[:, 1]
    pulled_a, pulled_b = parted(pulled)
    faded_a, faded_b = parted(faded)
    keys_a, keys_b = parted(keys)
    across = (half, half * (wide // HSIZE))
    same = (
        lax.broadcasted_iota(jnp.int32, across, 0) // size
        == lax.broadcasted_iota(jnp.int32, across, 1) % half // size
    )
    seen = jnp.where(same, dot_stacked(pulled_b, stack_split(faded_a), NT), 0.0)
    moved = scaled(pulled_b, gain_a) - dot_stacked(seen, stack_split(pulled_a), NN)
    hit = jnp.where(same, dot_stacked(keys_a, stack_split(pulled_b), NT), 0.0)
    kept = scaled(keys_a, gain_b) - dot_stacked(hit, stack_split(faded_b), NN)
    return (
        gain_a * gain_b,
        joined(pulled_a, moved),
        joined(scaled(faded_a, gain_b), faded_b),
        joined(kept, keys_b),
    )


def state_group(prefix, answers, ones, diag_block):
    key, value, kappa, decay, learn = prefix
    query, akey, avalue, akappa, adecay, alearn = answers
    rows, wide = key.shape
    arows = query.shape[0]
    retain, unit, removal = factors(
        jnp.concatenate([kappa, akappa], 0),
        jnp.concatenate([decay, adecay], 0),
        jnp.concatenate([learn, alearn], 0),
        ones,
    )

    def tiled(x):
        return x.reshape(-1, 8, wide)

    tiles = rows // 8
    aretain, aunit, aremoval = [tiled(x[rows:]) for x in (retain, unit, removal)]
    retain, unit, removal = [tiled(x[:rows]) for x in (retain, unit, removal)]
    akey, avalue = tiled(akey.astype(F32)), tiled(avalue.astype(F32))
    sub = lax.broadcasted_iota(jnp.int32, (tiles, 8, wide), 1)
    asub = sub[: arows // 8]
    pushed = tiled(key.astype(F32))
    pulled = unit
    apulled = tiled(query.astype(F32))
    out = jnp.zeros_like(apulled)
    for t in range(8):
        j = 7 - t
        pt = slice(t, t + 1)
        aj = slice(j, j + 1)
        terms = [apulled * akey[:, aj], apulled * aremoval[:, aj]]
        if t == 0:
            terms = [x.reshape(-1, wide) for x in terms]
            sums = head_sum(jnp.concatenate(terms, 0), ones)
            got, gone = tiled(sums[:arows]), tiled(sums[arows:])
        if t > 0:
            pj = slice(7 - t, 8 - t)
            terms = [pushed * unit[:, pt], pulled * removal[:, pj]] + terms
            terms = [x.reshape(-1, wide) for x in terms]
            sums = head_sum(jnp.concatenate(terms, 0), ones)
            new = pushed * retain[:, pt] - tiled(sums[:rows]) * removal[:, pt]
            pushed = jnp.where(sub < t, new, pushed)
            new = pulled * retain[:, pj] - tiled(sums[rows : 2 * rows]) * unit[:, pj]
            pulled = jnp.where(sub > 7 - t, new, pulled)
            got = tiled(sums[2 * rows : 2 * rows + arows])
            gone = tiled(sums[2 * rows + arows :])
        live = asub >= j
        out = out + jnp.where(live, got * avalue[:, aj], 0.0)
        apulled = jnp.where(live, apulled * aretain[:, aj] - gone * aunit[:, aj], apulled)
    gain = jnp.ones((tiles, 1, wide), F32)
    faded = removal
    for t in range(7, -1, -1):
        faded = jnp.where(sub == t, removal * gain, faded)
        gain = gain * retain[:, t : t + 1]
    pulled, faded, keys = [x.reshape(rows, wide) for x in (pulled, faded, pushed)]
    size = 8
    while size < rows:
        gain, pulled, faded, keys = merge(gain, pulled, faded, keys, size)
        size *= 2
    gain = gain.reshape(1, wide)
    low_rank = fold_heads(jnp.where(diag_block, dot3(pulled, faded, TN), 0.0))
    eye = (
        lax.broadcasted_iota(jnp.int32, (HSIZE, wide), 0)
        == lax.broadcasted_iota(jnp.int32, (HSIZE, wide), 1) % HSIZE
    )
    passage = jnp.where(eye, gain, 0.0) - low_rank
    high, low = split(keys)
    outer = mm(value, high, TN) + mm(value, low, TN)
    update = fold_heads(jnp.where(diag_block, outer, 0.0))
    return passage, update, apulled.reshape(arows, wide), out.reshape(arows, wide)


def documents(lengths, moves):
    shards = moves.shape[0]
    docs = lengths.shape[0]
    starts = []
    total = jnp.int32(0)
    for d in range(docs):
        starts.append(total)
        total = total + lengths[d]
    now = [moves[jnp.minimum(starts[d], shards - 1), HSIZE : 2 * HSIZE] for d in range(docs)]

    def step(j, now):
        out = []
        for d in range(docs):
            at = jnp.minimum(starts[d] + j, shards - 1)
            new = dot3(now[d], stack_heads(moves[at, :HSIZE])) + moves[at, HSIZE : 2 * HSIZE]
            out.append(jnp.where(j < lengths[d], new, now[d]))
        return out

    return [x.astype(BF16) for x in lax.fori_loop(1, shards // 2, step, now)]


def flip(a, b, bits):
    total = 0
    for j in range(bits):
        one = 2**j
        total = total + (a // one + b // one) % 2 * one
    return total


def hidden_rows(docs, asked, query, fresh, ones):
    high, low = split(query)
    keep = [jnp.where(asked == d, 1.0, 0.0).astype(BF16) for d in range(len(docs))]
    masked = [jnp.concatenate([part * k for k in keep], 1) for part in (high, low)]
    memory = jnp.concatenate([stack_heads(x.astype(F32)).astype(BF16) for x in docs], 1)
    rows = query.shape[0]
    both = mm(jnp.concatenate(masked, 0), memory, NT)
    out = both[:rows] + (both[rows:] + fresh)
    centre = out - head_sum(out, ones) * (1.0 / HSIZE)
    spread = head_sum(centre * centre, ones) * (1.0 / HSIZE)
    return (centre * lax.rsqrt(spread + 1e-05)).astype(BF16)


def score_kernel(copies, kept, lengths, question_doc, tokens, choice_lengths, *refs):
    (
        prefix_hbm,
        answers_hbm,
        weight,
        scores,
        prefix,
        answers,
        moves,
        moves_all,
        query_rows,
        fresh_rows,
        asked_rows,
        id_rows,
        rows_all,
        weight_all,
        sums,
        stats,
        stats_all,
        peak,
        mass,
        picked,
        in_sem,
        weight_sem,
        move_send,
        move_recv,
        far_send,
        far_recv,
        mid_send,
        mid_recv,
        near_send,
        near_recv,
        stat_send,
        stat_recv,
    ) = (refs[:5], refs[5:11]) + refs[11:13] + (refs[13:18], refs[18:24]) + refs[24:]
    shards = moves_all.shape[0]
    units = moves.shape[0]
    me = lax.axis_index("seq")
    rows = answers[0].shape[0]
    tiles, _, tile = weight_all.shape
    choices = choice_lengths.shape[1]
    slots = rows // choices
    total = shards * kept
    per_turn = 4
    turns = units // per_turn
    bits = turns.bit_length() - 1
    span = per_turn * LANES
    my_unit = me // copies
    my_turn = my_unit // per_turn

    def fetch_in(turn):
        s = pl.ds(pl.multiple_of(flip(my_turn, turns - 1 - turn, bits) * span, span), span)
        return [
            pltpu.make_async_copy(source.at[:, s], target.at[:, s], in_sem.at[turn, a])
            for a, (source, target) in enumerate(
                zip(prefix_hbm + answers_hbm, prefix + answers)
            )
        ]

    for turn in range(turns):
        for copy in fetch_in(turn):
            copy.start()

    def fetch(i):
        return pltpu.make_async_copy(
            weight.at[:, pl.ds(i * tile, tile)], weight_all.at[i], weight_sem.at[i]
        )

    def plan(source, target, send_sem, recv_sem, dest):
        return pltpu.make_async_remote_copy(
            src_ref=source,
            dst_ref=target,
            send_sem=send_sem,
            recv_sem=recv_sem,
            device_id={"seq": dest},
            device_id_type=pl.DeviceIdType.MESH,
        )

    def send(*route):
        copy = plan(*route)
        copy.start()
        return copy

    barrier = pltpu.get_barrier_semaphore()
    for k in range(1, shards):
        pl.semaphore_signal(
            barrier,
            inc=1,
            device_id={"seq": lax.rem(me + k, shards)},
            device_id_type=pl.DeviceIdType.MESH,
        )
    for i in range(tiles):
        fetch(i).start()

    starts = [jnp.int32(0)]
    for c in range(choices):
        starts.append(starts[c] + choice_lengths[0, c])

    lane = lax.broadcasted_iota(jnp.int32, (8, LANES), 1)
    meta = jnp.where(lane == kept, question_doc[0], 0)
    for c in range(choices):
        for j in range(slots):
            spot = jnp.where(j < choice_lengths[0, c], starts[c] + j, -1)
            meta = jnp.where(lane == spot, tokens[0, c, j], meta)
    meta = meta.astype(F32)

    at = lax.broadcasted_iota(jnp.int32, (2 * kept, 2 * rows), 0)
    part = at // kept
    at = at - part * kept
    wanted = part * rows + at
    for c in range(1, choices):
        wanted = wanted + jnp.where(at >= starts[c], slots - choice_lengths[0, c - 1], 0)
    column = lax.broadcasted_iota(jnp.int32, (2 * kept, 2 * rows), 1)
    choose = jnp.where(column == wanted, 1.0, 0.0).astype(BF16)

    def move(unit, source, peer):
        return plan(
            moves.at[unit], moves_all.at[source], move_send.at[peer], move_recv.at[source], peer
        )

    diag_block = block_mask(WIDE, WIDE)
    wide_ones = jnp.where(diag_block, 1.0, 0.0).astype(BF16)
    per_group = WIDE // LANES

    def state_step(i, carry):
        turn = flip(my_turn, turns - 1 - i, bits)
        for copy in fetch_in(i):
            copy.wait()
        for g in range(2):
            s = pl.ds(pl.multiple_of(turn * span + g * WIDE, WIDE), WIDE)
            passage, update, q, o = state_group(
                [r[:, s] for r in prefix], [r[:, s] for r in answers], wide_ones, diag_block
            )
            both = jnp.concatenate(split(jnp.concatenate([q, o], 0)), 1)
            both = mm(choose, both, NN)
            both = both[:, :WIDE] + both[:, WIDE:]
            for u in range(per_group):
                lanes = slice(u * LANES, (u + 1) * LANES)
                unit = turn * per_turn + g * per_group + u
                moves[unit, :HSIZE] = passage[:, lanes]
                moves[unit, HSIZE : 2 * HSIZE] = update[:, lanes]
                moves[unit, 2 * HSIZE : 2 * HSIZE + 2 * kept] = both[:, lanes]
                moves[unit, 2 * HSIZE + 2 * kept :] = meta

        @pl.when(i == 0)
        def _():
            pl.semaphore_wait(barrier, shards - 1)

        for u in range(per_turn):
            unit = turn * per_turn + u
            for c in range(copies):
                peer = unit * copies + c

                @pl.when(peer != me)
                def _():
                    move(unit, me, peer).start()

        return carry

    with jax.named_scope("state"):
        lax.fori_loop(0, turns, state_step, 0)
        moves_all[me] = moves[my_unit]
    with jax.named_scope("moves"):
        for source in range(shards):

            @pl.when(source != me)
            def _():
                move(source // copies, source, source).wait_recv()

    with jax.named_scope("documents"):
        docs = documents(lengths, moves_all)
    with jax.named_scope("hidden"):
        for q in range(shards):
            s = slice(q * kept, (q + 1) * kept)
            low = 2 * HSIZE
            query_rows[s, :] = moves_all[q, low : low + kept]
            fresh_rows[s, :] = moves_all[q, low + kept : low + 2 * kept]
            line = moves_all[q, low + 2 * kept : low + 2 * kept + 1, :]
            line = jnp.broadcast_to(line, (kept, LANES))
            lane = lax.broadcasted_iota(jnp.int32, (kept, LANES), 1)
            here = lax.broadcasted_iota(jnp.int32, (kept, LANES), 0)
            ids = jnp.sum(jnp.where(lane == here, line, 0.0), 1, keepdims=True)
            asked = jnp.sum(jnp.where(lane == kept, line, 0.0), 1, keepdims=True)
            id_rows[s, :] = jnp.broadcast_to(ids, (kept, LANES)).astype(jnp.int32)
            asked_rows[s, :] = jnp.broadcast_to(asked, (kept, LANES)).astype(jnp.int32)
        ones = jnp.where(block_mask(LANES, LANES), 1.0, 0.0).astype(BF16)
        rows_all[my_unit] = hidden_rows(
            docs, asked_rows[...], query_rows[...], fresh_rows[...], ones
        )

    first = me * (tiles * tile)

    def chunk(place):
        depth = pl.ds(pl.multiple_of(place * span, span), span)
        parts = [rows_all[place * per_turn + u] for u in range(per_turn)]
        return jnp.concatenate(parts, 1), depth

    def start_sums(place):
        with jax.named_scope("logits"):
            left, depth = chunk(place)

            def step(i, carry):
                if place is places[0]:
                    fetch(i).wait()
                add = jnp.dot(left, weight_all[i, depth, :], preferred_element_type=F32)
                sums[i] = add if place is places[0] else sums[i] + add
                return carry

            lax.fori_loop(0, tiles, step, 0)

    sent = []
    places = [flip(my_turn, d, bits) for d in range(turns)]
    if copies == 1:
        place = lax.rem(me, 4)
        mid_peer = me + 2 - 4 * (place // 2)
        near_peer = me + 1 - 2 * lax.rem(me, 2)
        other = lax.rem(place + 2, 4)

        def pass_on(slot, send_sems, recv_sems, k, dest):
            copy = send(rows_all.at[slot], rows_all.at[slot], send_sems.at[k], recv_sems.at[k], dest)
            sent.append(copy)
            return copy

        fars = [None]
        for d in range(1, turns):
            fars.append(pass_on(me, far_send, far_recv, d, places[d] * 4 + place))
        mids = [pass_on(me, mid_send, mid_recv, 0, mid_peer)]
        nears = [pass_on(me, near_send, near_recv, 0, near_peer)]
        for d in range(turns):
            with jax.named_scope("gather"):
                mids[d].wait_recv()
                later = pass_on(
                    places[d] * 4 + other, near_send, near_recv, turns + d, near_peer
                )
                if d + 1 < turns:
                    fars[d + 1].wait_recv()
                    slot = places[d + 1] * 4 + place
                    mids.append(pass_on(slot, mid_send, mid_recv, d + 1, mid_peer))
                    nears.append(pass_on(slot, near_send, near_recv, d + 1, near_peer))
                nears[d].wait_recv()
                later.wait_recv()
            if d + 1 < turns:
                start_sums(places[d])
    else:
        lead = lax.rem(me, copies)
        arriving = []
        for d in range(1, units):
            dest = lax.rem(my_unit + d, units) * copies + lead
            arriving.append(
                send(
                    rows_all.at[my_unit], rows_all.at[my_unit], far_send.at[d], far_recv.at[d], dest
                )
            )
        for copy in arriving:
            copy.wait_recv()
        sent += arriving
        for d in range(turns - 1):
            start_sums(places[d])

    peak[...] = jnp.full_like(peak, -jnp.inf)
    mass[...] = jnp.zeros_like(mass)
    picked[...] = jnp.zeros_like(picked)
    left, depth = chunk(places[-1])

    def score_tile(i, carry):
        logits = sums[i] + jnp.dot(left, weight_all[i, depth, :], preferred_element_type=F32)
        parts = [logits[:, p * LANES : (p + 1) * LANES] for p in range(tile // LANES)]
        old = peak[...]
        new = functools.reduce(jnp.maximum, parts, old)
        add = mass[...] * jnp.exp(old - new)
        pick = picked[...]
        lane = lax.broadcasted_iota(jnp.int32, (total, LANES), 1) - id_rows[...]
        for p, part in enumerate(parts):
            add = add + jnp.exp(part - new)
            pick = pick + jnp.where(lane == -(first + i * tile + p * LANES), part, 0.0)
        peak[...] = new
        mass[...] = add
        picked[...] = pick
        return carry

    with jax.named_scope("scores"):
        lax.fori_loop(0, tiles, score_tile, 0)
    with jax.named_scope("stats"):
        top = jnp.max(peak[...], 1, keepdims=True)
        summed = jnp.sum(mass[...] * jnp.exp(peak[...] - top), 1, keepdims=True)
        chosen = jnp.sum(picked[...], 1, keepdims=True)
        lane = lax.broadcasted_iota(jnp.int32, (total, LANES), 1)
        packed = jnp.where(lane == 0, top, jnp.where(lane == 1, summed, chosen))
        short = -total % LANES
        if short:
            packed = jnp.concatenate([packed, jnp.zeros((short, LANES), F32)], 0)
        flat = jnp.concatenate(
            [
                jnp.transpose(packed[b * LANES : (b + 1) * LANES])[:8]
                for b in range((total + short) // LANES)
            ],
            1,
        )
        for q in range(shards):
            low = q * kept // LANES * LANES
            two = flat[:, low : min(low + 2 * LANES, flat.shape[1])]
            back = q * kept - low
            if back:
                two = pltpu.roll(two, two.shape[1] - back, 1)
            stats[q] = two[:, :LANES]

        arriving = []
        for k in range(1, shards):
            dest = lax.rem(me + k, shards)
            arriving.append(
                send(stats.at[dest], stats_all.at[me], stat_send.at[k], stat_recv.at[k], dest)
            )
        stats_all[me] = stats[me]
        for copy in arriving:
            copy.wait_recv()
        sent += arriving
    tops = stats_all[:, 0:1, :]
    overall = jnp.max(tops, 0)
    masses = jnp.sum(stats_all[:, 1:2, :] * jnp.exp(tops - overall[None]), 0)
    logprob = jnp.sum(stats_all[:, 2:3, :], 0) - (overall + jnp.log(masses))
    lane = lax.broadcasted_iota(jnp.int32, (1, LANES), 1)
    result = jnp.zeros((1, LANES), F32)
    for c in range(choices):
        mine = jnp.where((lane >= starts[c]) & (lane < starts[c + 1]), logprob, 0.0)
        count = jnp.full((1, LANES), choice_lengths[0, c], jnp.int32).astype(F32)
        result = jnp.where(lane == c, jnp.sum(mine, 1, keepdims=True) / count, result)
    scores[...] = result[:, :choices]
    with jax.named_scope("sent"):
        for copy in sent:
            copy.wait_send()
        for peer in range(shards):

            @pl.when(peer != me)
            def _():
                move(peer // copies, me, peer).wait_send()


VMEM = pl.BlockSpec(memory_space=pltpu.VMEM)
SMEM = pl.BlockSpec(memory_space=pltpu.SMEM)
ANY = pl.BlockSpec(memory_space=pl.ANY)


def local(*args):
    prefix, answers = args[:5], args[5:11]
    doc_lengths, question_doc, choice_tokens, choice_lengths, head_weight = args[11:]
    shards = lax.axis_size("seq")
    tok_rows, width = prefix[0].shape
    answers = [a.reshape(-1, width) for a in answers]
    rows = answers[0].shape[0]
    kept = rows * 5 // 8
    units = width // LANES
    copies = max(shards // units, 1)
    vocab_dev = head_weight.shape[1]
    tile = 512
    tiles = vocab_dev // tile
    total = shards * kept
    message = 2 * HSIZE + 2 * kept + 8
    choices = choice_tokens.shape[1]
    dma = pltpu.SemaphoreType.DMA
    return pl.pallas_call(
        functools.partial(score_kernel, copies, kept),
        in_specs=[SMEM] * 4 + [ANY] * 12,
        out_specs=VMEM,
        out_shape=jax.ShapeDtypeStruct((1, choices), F32),
        scratch_shapes=[pltpu.VMEM((tok_rows, width), BF16)] * 5
        + [pltpu.VMEM((rows, width), BF16)] * 6
        + [
            pltpu.VMEM((units, message, LANES), F32),
            pltpu.VMEM((shards, message, LANES), F32),
            pltpu.VMEM((total, LANES), F32),
            pltpu.VMEM((total, LANES), F32),
            pltpu.VMEM((total, LANES), jnp.int32),
            pltpu.VMEM((total, LANES), jnp.int32),
            pltpu.VMEM((units, total, LANES), BF16),
            pltpu.VMEM((tiles, width, tile), BF16),
            pltpu.VMEM((tiles, total, tile), F32),
            pltpu.VMEM((shards, 8, LANES), F32),
            pltpu.VMEM((shards, 8, LANES), F32),
            pltpu.VMEM((total, LANES), F32),
            pltpu.VMEM((total, LANES), F32),
            pltpu.VMEM((total, LANES), F32),
            dma((units // 4, 11)),
            dma((tiles,)),
        ]
        + [dma((shards,))] * 10,
        compiler_params=pltpu.CompilerParams(
            vmem_limit_bytes=60 * 2**20, collective_id=0, has_side_effects=True
        ),
        name="score",
    )(doc_lengths, question_doc, choice_tokens, choice_lengths, *prefix, *answers, head_weight)


def solution(mesh):
    token = P(("group", "seq"), None)
    choice = P(("group", "seq"), None, None, None)
    placed = (token,) * 5 + (choice,) * 6
    placed += (
        P("group"),
        P(("group", "seq")),
        P(("group", "seq"), None, None),
        P(("group", "seq"), None),
        P(None, "seq"),
    )
    return jax.shard_map(
        local, mesh=mesh, in_specs=placed, out_specs=P(("group", "seq"), None), check_vma=False
    )
```
